32 devices in a mesh: scene: 4 (over x, core), view: 4 (over z), half: 2 (over y).
Axes of the slice: x: 2, y: 2, z: 4, core: 2. Of those that a mesh axis runs over, the one named last changes fastest.
Arguments:
- tokens: bfloat16 [16, 512, 2048], P(('scene', 'view'), 'half'), parts along dimension 0, may hold values from -9 to 12
- w_qkv: bfloat16 [2048, 768], replicated, may hold values from -0.125 to 0.125
- w_out: bfloat16 [256, 2048], replicated, may hold values from -5 to 5
- key_lists: int32 [16, 4, 2], P(('scene', 'view'), 'half'), parts along dimension 0, may hold values from 0 to 15, as said below
- list_len: int32 [16, 4], P(('scene', 'view'), 'half'), parts along dimension 0, may hold values from 1 to 2, as said below
Outputs:
- mixed: bfloat16 [16, 512, 2048], P(('scene', 'view'), 'half'), parts along dimension 0
The draws below stay inside these ranges and needn't reach their ends.
There are 4 independent parts, one for each index of `scene`. The reference program is written for one: setup_inputs(seed, part) draws one part's arguments, and reference() takes and returns one part's arrays. A program takes and returns all parts, laid end to end along the dimension named above; an argument that names none is the same for every part. Nothing has to cross between parts.
Inputs may be any that keep to these rules, and one draw needn't show every extreme that they name: `key_lists`: entries of one list are distinct block ids of the scene. `list_len`: some query block lists 2 blocks in every scene.
All inputs are finite; a program needn't handle non-finite values.
Results may differ from the reference program's by a relative error of at most 0.014.
The reference program's roundings to bfloat16 on the way (of `proj` and `attn`) count: a program that leaves them out, or rounds other values in their place, can miss the bound.
Values may be sent and summed in bfloat16 or wider, within the bound.
A program may use at most 64 MiB of HBM per device.

```python
import jax
import jax.numpy as jnp
from jax import lax

D = 2048
HEADS = 4
HD = 64
BLK = 128
TOKV = 512
VIEWS = 4
LMAX = 2


def draw_tokens(key, part):
    first = jax.random.fold_in(key, 0)
    shape = (VIEWS, TOKV, D)
    return jnp.clip(jax.random.normal(first, shape, jnp.float32), -6.0, 6.0).astype(jnp.bfloat16)


def draw_key_lists(key, part):
    blocks = VIEWS * TOKV // BLK
    raw = jax.random.randint(key, (blocks, blocks), 0, 65536)
    ranked = raw * blocks + jnp.arange(blocks, dtype=jnp.int32)[None, :]
    unused, picked = lax.top_k(ranked, LMAX)
    return picked.astype(jnp.int32).reshape(VIEWS, TOKV // BLK, LMAX)


def draw_list_len(key, part):
    blocks = VIEWS * TOKV // BLK
    lengths = jax.random.randint(key, (blocks,), 1, LMAX + 1)
    lengths = jnp.where(jnp.arange(blocks, dtype=jnp.int32) == 0, LMAX, lengths)
    return lengths.astype(jnp.int32).reshape(VIEWS, TOKV // BLK)


def gaussian(rng, shape, scale, most, held_as=jnp.bfloat16):
    array = scale * jax.random.normal(rng, shape, jnp.float32)
    return jnp.clip(array, min=-most, max=most).astype(held_as)


def setup_inputs(seed: int = 0, part: int = 0) -> dict:
    splits = jax.random.split(jax.random.key(seed), 6)
    own_keys = jax.random.split(jax.random.fold_in(splits[5], part), 6)
    return {
        "tokens": draw_tokens(jax.random.fold_in(jax.random.fold_in(splits[5], part), 71), part),
        "w_qkv": gaussian(splits[1], (D, 3 * HEADS * HD), D ** -0.5, 0.125),
        "w_out": gaussian(splits[2], (HEADS * HD, D), 1.0, 5.0),
        "key_lists": draw_key_lists(jax.random.fold_in(jax.random.fold_in(splits[5], part), 71), part),
        "list_len": draw_list_len(jax.random.fold_in(jax.random.fold_in(splits[5], part), 71), part),
    }


NEG = -1.0e30


def reference(tokens, w_qkv, w_out, key_lists, list_len):
    views, tokv, width = tokens.shape
    count = views * tokv
    flat = tokens.reshape(count, width)
    inner = w_out.shape[0]
    head_size = inner // HEADS
    proj = jnp.dot(flat, w_qkv, preferred_element_type=jnp.float32).astype(jnp.bfloat16)
    queries = proj[:, :inner]
    keys = proj[:, inner:2 * inner].reshape(count, HEADS, head_size).astype(jnp.float32)
    values = proj[:, 2 * inner:].reshape(count, HEADS, head_size).astype(jnp.float32)
    nblocks = count // BLK
    lists = key_lists.reshape(nblocks, -1)
    lengths = list_len.reshape(nblocks)
    slots = jnp.arange(lists.shape[1], dtype=jnp.int32)
    live = slots[None, :] < lengths[:, None]
    ids = jnp.arange(nblocks, dtype=jnp.int32)
    allowed = jnp.any((lists[:, :, None] == ids[None, None, :]) & live[:, :, None], axis=1)

    def one_block(item):
        block_q, mask = item
        keymask = jnp.repeat(mask, BLK)
        q3 = block_q.reshape(BLK, HEADS, head_size).astype(jnp.float32)
        scores = jnp.einsum("qhd,khd->hqk", q3, keys) * (head_size ** -0.5)
        masked = jnp.where(keymask[None, None, :], scores, NEG)
        top = jnp.max(masked, axis=2, keepdims=True)
        weights = jnp.where(keymask[None, None, :], jnp.exp(scores - top), 0.0)
        total = jnp.sum(weights, axis=2)
        rounded = lax.optimization_barrier(weights.astype(jnp.bfloat16)).astype(jnp.float32)
        summed = jnp.einsum("hqk,khd->qhd", rounded, values)
        return (summed / total.T[:, :, None]).reshape(BLK, inner).astype(jnp.bfloat16)

    attn = lax.map(one_block, (queries.reshape(nblocks, BLK, inner), allowed)).reshape(count, inner)
    mixed = jnp.dot(attn, w_out, preferred_element_type=jnp.float32).astype(jnp.bfloat16)
    return mixed.reshape(views, tokv, width)
```

```python
import functools

import jax
import jax.numpy as jnp
from jax import lax
from jax.experimental import pallas as pl
from jax.experimental.pallas import tpu as pltpu
from jax.sharding import PartitionSpec as P

HEADS = 4
NEG = -1e30
MESH = pl.DeviceIdType.MESH


def body(
    sizes,
    lists_ref,
    lens_ref,
    tokens_ref,
    w_ref,
    w_out_ref,
    out_ref,
    x,
    w,
    wo,
    kbuf,
    vbuf,
    weight_buf,
    total_buf,
    load_sem,
    send_sem,
    recv_sem,
):
    views, halves = sizes
    view, half = lax.axis_index("view"), lax.axis_index("half")
    count, block, inner = kbuf.shape
    local = count // (views * halves)
    rows = local * block
    head_size = inner // HEADS
    slots = lists_ref.shape[1]
    bufs = (kbuf, vbuf)

    loads = [pltpu.make_async_copy(tokens_ref, x, load_sem.at[0])]
    for n, group in enumerate((1, 2, 0)):
        cols = pl.ds(group * inner, inner)
        loads.append(
            pltpu.make_async_copy(w_ref.at[:, cols], w.at[group], load_sem.at[1 + n])
        )
    loads.append(pltpu.make_async_copy(w_out_ref, wo, load_sem.at[4]))
    for load in loads:
        load.start()

    toward = (
        (view + 1 < views, {"view": view + 1}, views),
        (view >= 1, {"view": view - 1}, views),
        (half + 1 < halves, {"half": half + 1}, halves),
        (half >= 1, {"half": half - 1}, halves),
    )

    barrier = pltpu.get_barrier_semaphore()
    for there, device, size in toward:
        if size > 1:

            @pl.when(there)
            def _():
                pl.semaphore_signal(barrier, inc=1, device_id=device, device_id_type=MESH)

    def piece(c, slot, way):
        rows_of = bufs[c].at[pl.ds(slot * local, local)]
        return pltpu.make_async_remote_copy(
            src_ref=rows_of,
            dst_ref=rows_of,
            send_sem=send_sem.at[way, c, slot],
            recv_sem=recv_sem.at[c, slot],
            device_id=toward[way][1],
            device_id_type=MESH,
        )

    sends = []

    def send(c, slot, way, here):
        there, _, size = toward[way]
        if size == 1:
            return
        cond = there if here is None else jnp.logical_and(here, there)
        sends.append((cond, c, slot, way))

        @pl.when(cond)
        def _():
            piece(c, slot, way).start()

    def arrive(c, slot, here):
        @pl.when(here)
        def _():
            piece(c, slot, 0).wait_recv()

    def project(group):
        return jnp.dot(x[...], w[group], preferred_element_type=jnp.float32).astype(
            jnp.bfloat16
        )

    own = view * halves + half
    loads[0].wait()
    for c in range(2):
        loads[1 + c].wait()
        bufs[c][pl.ds(own * local, local)] = project(1 + c).reshape(local, block, inner)
        if c == 0:
            expected = sum(there.astype(jnp.int32) for there, _, size in toward if size > 1)
            pl.semaphore_wait(barrier, expected)
        for way in (2, 3, 0, 1):
            send(c, own, way, None)

    loads[3].wait()
    queries = project(0)
    head_of = lax.broadcasted_iota(jnp.int32, (block, inner), 1) // head_size
    mine = [head_of == h for h in range(HEADS)]

    def along_view(c, dist):
        for sign, way in ((-1, 0), (1, 1)):
            shard = view + sign * dist
            here = shard >= 0 if sign < 0 else shard < views
            slot = shard * halves + half
            arrive(c, slot, here)
            for out in (2, 3):
                send(c, slot, out, here)
            if dist + 1 < views:
                send(c, slot, way, here)

    def along_half(c):
        for far in range(1, halves):
            for dist in range(views):
                for sign in (-1, 1) if dist else (1,):
                    shard = view + sign * dist
                    seen = shard >= 0 if sign < 0 else shard < views
                    for side, way in ((-1, 2), (1, 3)):
                        other = half + side * far
                        here = jnp.logical_and(seen, other >= 0 if side < 0 else other < halves)
                        slot = shard * halves + other
                        arrive(c, slot, here)
                        if far + 1 < halves:
                            send(c, slot, way, here)

    order = [(c, 1) for c in range(2)]
    order += [(c, dist) for c in range(2) for dist in range(2, views)]
    for c, dist in order:
        if dist < views:
            along_view(c, dist)

    along_half(0)
    for i in range(local):
        q = queries[i * block : (i + 1) * block]
        stacked = jnp.concatenate([jnp.where(m, q, jnp.zeros_like(q)) for m in mine], axis=0)
        keys = jnp.concatenate([kbuf[lists_ref[i, s]] for s in range(slots)], axis=0)
        scores = lax.dot_general(
            stacked, keys, (((1,), (1,)), ((), ())), preferred_element_type=jnp.float32
        ) * head_size ** (-0.5)
        live = lax.broadcasted_iota(jnp.int32, scores.shape, 1) // block < lens_ref[i]
        top = jnp.max(jnp.where(live, scores, NEG), axis=1, keepdims=True)
        weights = jnp.where(live, jnp.exp(scores - top), 0.0)
        total_buf[i] = jnp.sum(weights, axis=1, keepdims=True)
        weight_buf[i] = weights.astype(jnp.bfloat16)

    along_half(1)
    loads[4].wait()
    for i in range(local):
        values = jnp.concatenate([vbuf[lists_ref[i, s]] for s in range(slots)], axis=0)
        summed = jnp.dot(weight_buf[i], values, preferred_element_type=jnp.float32)
        scaled = summed / total_buf[i]
        attn = jnp.zeros((block, inner), jnp.float32)
        for h, m in enumerate(mine):
            attn = jnp.where(m, scaled[h * block : (h + 1) * block], attn)
        out_ref[i * block : (i + 1) * block] = jnp.dot(
            attn.astype(jnp.bfloat16), wo[...], preferred_element_type=jnp.float32
        ).astype(out_ref.dtype)

    for cond, c, slot, way in sends:

        @pl.when(cond)
        def _():
            piece(c, slot, way).wait_send()


def per_device(sizes, tokens, w_qkv, w_out, key_lists, list_len):
    views, halves = sizes
    rows, width = tokens.shape[1:]
    inner = w_out.shape[0]
    local = key_lists.shape[1]
    slots = key_lists.shape[2]
    block = rows // local
    shards = views * halves
    anywhere = pl.BlockSpec(memory_space=pl.ANY)
    mixed = pl.pallas_call(
        functools.partial(body, sizes),
        out_shape=jax.ShapeDtypeStruct((rows, width), jnp.bfloat16),
        in_specs=[
            pl.BlockSpec(memory_space=pltpu.SMEM),
            pl.BlockSpec(memory_space=pltpu.SMEM),
            anywhere,
            anywhere,
            anywhere,
        ],
        out_specs=pl.BlockSpec(memory_space=pltpu.VMEM),
        scratch_shapes=[
            pltpu.VMEM((rows, width), jnp.bfloat16),
            pltpu.VMEM((3, width, inner), jnp.bfloat16),
            pltpu.VMEM((inner, width), jnp.bfloat16),
            pltpu.VMEM((shards * local, block, inner), jnp.bfloat16),
            pltpu.VMEM((shards * local, block, inner), jnp.bfloat16),
            pltpu.VMEM((local, HEADS * block, slots * block), jnp.bfloat16),
            pltpu.VMEM((local, HEADS * block, 1), jnp.float32),
            pltpu.SemaphoreType.DMA((5,)),
            pltpu.SemaphoreType.DMA((4, 2, shards)),
            pltpu.SemaphoreType.DMA((2, shards)),
        ],
        compiler_params=pltpu.CompilerParams(collective_id=0, has_side_effects=True),
    )(
        key_lists.reshape(local, slots),
        list_len.reshape(local),
        tokens.reshape(rows, width),
        w_qkv,
        w_out,
    )
    return mixed.reshape(1, rows, width)


def solution(mesh):
    sizes = (mesh.shape["view"], mesh.shape["half"])
    placed = (
        P(("scene", "view"), "half", None),
        P(),
        P(),
        P(("scene", "view"), "half", None),
        P(("scene", "view"), "half"),
    )
    return jax.shard_map(
        functools.partial(per_device, sizes),
        mesh=mesh,
        in_specs=placed,
        out_specs=P(("scene", "view"), "half", None),
        check_vma=False,
    )
```

```python
import functools

import jax
import jax.numpy as jnp
from jax import lax
from jax.experimental import pallas as pl
from jax.experimental.pallas import tpu as pltpu
from jax.sharding import PartitionSpec as P

HEADS = 4
NEG = -1e30
MESH = pl.DeviceIdType.MESH


def body(
    sizes,
    lists_ref,
    lens_ref,
    tokens_ref,
    w_ref,
    out_ref,
    x,
    w,
    kbuf,
    vbuf,
    weight_buf,
    total_buf,
    load_sem,
    send_sem,
    recv_sem,
):
    views, halves = sizes
    view, half = lax.axis_index("view"), lax.axis_index("half")
    count, block, inner = kbuf.shape
    local = count // (views * halves)
    rows = local * block
    head_size = inner // HEADS
    slots = lists_ref.shape[1]
    bufs = (kbuf, vbuf)

    loads = [pltpu.make_async_copy(tokens_ref, x, load_sem.at[0])]
    for n, group in enumerate((1, 2, 0)):
        cols = pl.ds(group * inner, inner)
        loads.append(
            pltpu.make_async_copy(w_ref.at[:, cols], w.at[group], load_sem.at[1 + n])
        )
    for load in loads:
        load.start()

    toward = (
        (view + 1 < views, {"view": view + 1}, views),
        (view >= 1, {"view": view - 1}, views),
        (half + 1 < halves, {"half": half + 1}, halves),
        (half >= 1, {"half": half - 1}, halves),
    )

    barrier = pltpu.get_barrier_semaphore()
    for there, device, size in toward:
        if size > 1:

            @pl.when(there)
            def _():
                pl.semaphore_signal(barrier, inc=1, device_id=device, device_id_type=MESH)

    def piece(c, slot, way):
        rows_of = bufs[c].at[pl.ds(slot * local, local)]
        return pltpu.make_async_remote_copy(
            src_ref=rows_of,
            dst_ref=rows_of,
            send_sem=send_sem.at[way, c, slot],
            recv_sem=recv_sem.at[c, slot],
            device_id=toward[way][1],
            device_id_type=MESH,
        )

    sends = []

    def send(c, slot, way, here):
        there, _, size = toward[way]
        if size == 1:
            return
        cond = there if here is None else jnp.logical_and(here, there)
        sends.append((cond, c, slot, way))

        @pl.when(cond)
        def _():
            piece(c, slot, way).start()

    def arrive(c, slot, here):
        @pl.when(here)
        def _():
            piece(c, slot, 0).wait_recv()

    def project(group):
        return jnp.dot(x[...], w[group], preferred_element_type=jnp.float32).astype(
            jnp.bfloat16
        )

    own = view * halves + half
    loads[0].wait()
    for c in range(2):
        loads[1 + c].wait()
        bufs[c][pl.ds(own * local, local)] = project(1 + c).reshape(local, block, inner)
        if c == 0:
            expected = sum(there.astype(jnp.int32) for there, _, size in toward if size > 1)
            pl.semaphore_wait(barrier, expected)
        for way in (2, 3, 0, 1):
            send(c, own, way, None)

    loads[3].wait()
    queries = project(0)
    head_of = lax.broadcasted_iota(jnp.int32, (block, inner), 1) // head_size
    mine = [head_of == h for h in range(HEADS)]

    def along_view(c, dist):
        for sign, way in ((-1, 0), (1, 1)):
            shard = view + sign * dist
            here = shard >= 0 if sign < 0 else shard < views
            slot = shard * halves + half
            arrive(c, slot, here)
            for out in (2, 3):
                send(c, slot, out, here)
            if dist + 1 < views:
                send(c, slot, way, here)

    def along_half(c):
        for far in range(1, halves):
            for dist in range(views):
                for sign in (-1, 1) if dist else (1,):
                    shard = view + sign * dist
                    seen = shard >= 0 if sign < 0 else shard < views
                    for side, way in ((-1, 2), (1, 3)):
                        other = half + side * far
                        here = jnp.logical_and(seen, other >= 0 if side < 0 else other < halves)
                        slot = shard * halves + other
                        arrive(c, slot, here)
                        if far + 1 < halves:
                            send(c, slot, way, here)

    order = [(c, 1) for c in range(2)]
    order += [(c, dist) for c in range(2) for dist in range(2, views)]
    for c, dist in order:
        if dist < views:
            along_view(c, dist)

    along_half(0)
    for i in range(local):
        q = queries[i * block : (i + 1) * block]
        stacked = jnp.concatenate([jnp.where(m, q, jnp.zeros_like(q)) for m in mine], axis=0)
        keys = jnp.concatenate([kbuf[lists_ref[i, s]] for s in range(slots)], axis=0)
        scores = lax.dot_general(
            stacked, keys, (((1,), (1,)), ((), ())), preferred_element_type=jnp.float32
        ) * head_size ** (-0.5)
        live = lax.broadcasted_iota(jnp.int32, scores.shape, 1) // block < lens_ref[i]
        top = jnp.max(jnp.where(live, scores, NEG), axis=1, keepdims=True)
        weights = jnp.where(live, jnp.exp(scores - top), 0.0)
        total_buf[i] = jnp.sum(weights, axis=1, keepdims=True)
        weight_buf[i] = weights.astype(jnp.bfloat16)

    along_half(1)
    for i in range(local):
        values = jnp.concatenate([vbuf[lists_ref[i, s]] for s in range(slots)], axis=0)
        summed = jnp.dot(weight_buf[i], values, preferred_element_type=jnp.float32)
        scaled = summed / total_buf[i]
        attn = jnp.zeros((block, inner), jnp.float32)
        for h, m in enumerate(mine):
            attn = jnp.where(m, scaled[h * block : (h + 1) * block], attn)
        out_ref[i * block : (i + 1) * block] = attn.astype(out_ref.dtype)

    for cond, c, slot, way in sends:

        @pl.when(cond)
        def _():
            piece(c, slot, way).wait_send()


def per_device(sizes, tokens, w_qkv, w_out, key_lists, list_len):
    views, halves = sizes
    rows, width = tokens.shape[1:]
    inner = w_out.shape[0]
    local = key_lists.shape[1]
    slots = key_lists.shape[2]
    block = rows // local
    shards = views * halves
    anywhere = pl.BlockSpec(memory_space=pl.ANY)
    attn = pl.pallas_call(
        functools.partial(body, sizes),
        out_shape=jax.ShapeDtypeStruct((rows, inner), jnp.bfloat16),
        in_specs=[
            pl.BlockSpec(memory_space=pltpu.SMEM),
            pl.BlockSpec(memory_space=pltpu.SMEM),
            anywhere,
            anywhere,
        ],
        out_specs=pl.BlockSpec(memory_space=pltpu.VMEM),
        scratch_shapes=[
            pltpu.VMEM((rows, width), jnp.bfloat16),
            pltpu.VMEM((3, width, inner), jnp.bfloat16),
            pltpu.VMEM((shards * local, block, inner), jnp.bfloat16),
            pltpu.VMEM((shards * local, block, inner), jnp.bfloat16),
            pltpu.VMEM((local, HEADS * block, slots * block), jnp.bfloat16),
            pltpu.VMEM((local, HEADS * block, 1), jnp.float32),
            pltpu.SemaphoreType.DMA((4,)),
            pltpu.SemaphoreType.DMA((4, 2, shards)),
            pltpu.SemaphoreType.DMA((2, shards)),
        ],
        compiler_params=pltpu.CompilerParams(collective_id=0, has_side_effects=True),
    )(
        key_lists.reshape(local, slots),
        list_len.reshape(local),
        tokens.reshape(rows, width),
        w_qkv,
    )
    mixed = jnp.dot(attn, w_out, preferred_element_type=jnp.float32).astype(jnp.bfloat16)
    return mixed.reshape(1, rows, width)


def solution(mesh):
    sizes = (mesh.shape["view"], mesh.shape["half"])
    placed = (
        P(("scene", "view"), "half", None),
        P(),
        P(),
        P(("scene", "view"), "half", None),
        P(("scene", "view"), "half"),
    )
    return jax.shard_map(
        functools.partial(per_device, sizes),
        mesh=mesh,
        in_specs=placed,
        out_specs=P(("scene", "view"), "half", None),
        check_vma=False,
    )
```

```python
import functools

import jax
import jax.numpy as jnp
from jax import lax
from jax.experimental import pallas as pl
from jax.experimental.pallas import tpu as pltpu
from jax.sharding import PartitionSpec as P

HEADS = 4
NEG = -1e30
MESH = pl.DeviceIdType.MESH


def body(
    sizes,
    lists_ref,
    lens_ref,
    tokens_ref,
    w_ref,
    out_ref,
    x,
    w,
    kbuf,
    vbuf,
    weight_buf,
    total_buf,
    load_sem,
    send_sem,
    recv_sem,
):
    views, halves = sizes
    view, half = lax.axis_index("view"), lax.axis_index("half")
    count, block, inner = kbuf.shape
    local = count // (views * halves)
    rows = local * block
    head_size = inner // HEADS
    slots = lists_ref.shape[1]
    bufs = (kbuf, vbuf)

    loads = [pltpu.make_async_copy(tokens_ref, x, load_sem.at[0])]
    for n, group in enumerate((1, 2, 0)):
        cols = pl.ds(group * inner, inner)
        loads.append(
            pltpu.make_async_copy(w_ref.at[:, cols], w.at[group], load_sem.at[1 + n])
        )
    for load in loads:
        load.start()

    toward = (
        (view + 1 < views, {"view": view + 1}, views),
        (view >= 1, {"view": view - 1}, views),
        (half + 1 < halves, {"half": half + 1}, halves),
        (half >= 1, {"half": half - 1}, halves),
    )

    barrier = pltpu.get_barrier_semaphore()
    for there, device, size in toward:
        if size > 1:

            @pl.when(there)
            def _():
                pl.semaphore_signal(barrier, inc=1, device_id=device, device_id_type=MESH)

    def piece(c, slot, way):
        rows_of = bufs[c].at[slot]
        return pltpu.make_async_remote_copy(
            src_ref=rows_of,
            dst_ref=rows_of,
            send_sem=send_sem.at[way, c, slot],
            recv_sem=recv_sem.at[c, slot],
            device_id=toward[way][1],
            device_id_type=MESH,
        )

    sends = []

    def send(c, slot, way, here):
        there, _, size = toward[way]
        if size == 1:
            return
        cond = there if here is None else jnp.logical_and(here, there)
        sends.append((cond, c, slot, way))

        @pl.when(cond)
        def _():
            piece(c, slot, way).start()

    def arrive(c, slot, here):
        @pl.when(here)
        def _():
            piece(c, slot, 0).wait_recv()

    def project(group):
        return jnp.dot(x[...], w[group], preferred_element_type=jnp.float32).astype(
            jnp.bfloat16
        )

    own = view * halves + half
    loads[0].wait()
    for c in range(2):
        loads[1 + c].wait()
        bufs[c][pl.ds(own * local, local)] = project(1 + c).reshape(local, block, inner)
        if c == 0:
            expected = sum(there.astype(jnp.int32) for there, _, size in toward if size > 1)
            pl.semaphore_wait(barrier, expected)
        for b in range(local):
            for way in (2, 3, 0, 1):
                send(c, own * local + b, way, None)

    loads[3].wait()
    queries = project(0)
    head_of = lax.broadcasted_iota(jnp.int32, (block, inner), 1) // head_size
    mine = [head_of == h for h in range(HEADS)]

    balanced = halves == 2 and views > 2

    def along_view(c, dist):
        for b in range(local):
            for sign, way in ((-1, 0), (1, 1)):
                shard = view + sign * dist
                here = shard >= 0 if sign < 0 else shard < views
                slot = (shard * halves + half) * local + b
                arrive(c, slot, here)
                across = here
                if balanced and c == 1 and dist == 1:
                    across = jnp.logical_and(here, view >= 1) if sign > 0 else None
                if across is not None:
                    for out in (2, 3):
                        send(c, slot, out, across)
                if dist + 1 < views:
                    send(c, slot, way, here)

    def along_half(c):
        for far in range(1, halves):
            for dist in range(1 if balanced and c == 1 else 0, views):
                for b in range(local):
                    for sign in (-1, 1) if dist else (1,):
                        shard = view + sign * dist
                        seen = shard >= 0 if sign < 0 else shard < views
                        for side, way in ((-1, 2), (1, 3)):
                            other = half + side * far
                            here = jnp.logical_and(
                                seen, other >= 0 if side < 0 else other < halves
                            )
                            slot = (shard * halves + other) * local + b
                            arrive(c, slot, here)
                            if far + 1 < halves:
                                send(c, slot, way, here)

    order = [(c, dist) for dist in range(1, views) for c in range(2)]
    for c, dist in order:
        along_view(c, dist)
    if balanced:
        for b in range(local):
            slot = (view * halves + (halves - 1) - half) * local + b
            arrive(1, slot, view >= 0)
            send(1, slot, 0, None)
            send(1, slot, 1, view == 1)

    along_half(0)
    for i in range(local):
        q = queries[i * block : (i + 1) * block]
        stacked = jnp.concatenate([jnp.where(m, q, jnp.zeros_like(q)) for m in mine], axis=0)
        keys = jnp.concatenate([kbuf[lists_ref[i, s]] for s in range(slots)], axis=0)
        scores = lax.dot_general(
            stacked, keys, (((1,), (1,)), ((), ())), preferred_element_type=jnp.float32
        ) * head_size ** (-0.5)
        live = lax.broadcasted_iota(jnp.int32, scores.shape, 1) // block < lens_ref[i]
        top = jnp.max(jnp.where(live, scores, NEG), axis=1, keepdims=True)
        weights = jnp.where(live, jnp.exp(scores - top), 0.0)
        total_buf[i] = jnp.sum(weights, axis=1, keepdims=True)
        weight_buf[i] = weights.astype(jnp.bfloat16)

    along_half(1)
    for i in range(local):
        values = jnp.concatenate([vbuf[lists_ref[i, s]] for s in range(slots)], axis=0)
        summed = jnp.dot(weight_buf[i], values, preferred_element_type=jnp.float32)
        scaled = summed / total_buf[i]
        attn = jnp.zeros((block, inner), jnp.float32)
        for h, m in enumerate(mine):
            attn = jnp.where(m, scaled[h * block : (h + 1) * block], attn)
        out_ref[i * block : (i + 1) * block] = attn.astype(out_ref.dtype)

    for cond, c, slot, way in sends:

        @pl.when(cond)
        def _():
            piece(c, slot, way).wait_send()


def per_device(sizes, tokens, w_qkv, w_out, key_lists, list_len):
    views, halves = sizes
    rows, width = tokens.shape[1:]
    inner = w_out.shape[0]
    local = key_lists.shape[1]
    slots = key_lists.shape[2]
    block = rows // local
    shards = views * halves
    anywhere = pl.BlockSpec(memory_space=pl.ANY)
    attn = pl.pallas_call(
        functools.partial(body, sizes),
        out_shape=jax.ShapeDtypeStruct((rows, inner), jnp.bfloat16),
        in_specs=[
            pl.BlockSpec(memory_space=pltpu.SMEM),
            pl.BlockSpec(memory_space=pltpu.SMEM),
            anywhere,
            anywhere,
        ],
        out_specs=pl.BlockSpec(memory_space=pltpu.VMEM),
        scratch_shapes=[
            pltpu.VMEM((rows, width), jnp.bfloat16),
            pltpu.VMEM((3, width, inner), jnp.bfloat16),
            pltpu.VMEM((shards * local, block, inner), jnp.bfloat16),
            pltpu.VMEM((shards * local, block, inner), jnp.bfloat16),
            pltpu.VMEM((local, HEADS * block, slots * block), jnp.bfloat16),
            pltpu.VMEM((local, HEADS * block, 1), jnp.float32),
            pltpu.SemaphoreType.DMA((4,)),
            pltpu.SemaphoreType.DMA((4, 2, shards * local)),
            pltpu.SemaphoreType.DMA((2, shards * local)),
        ],
        compiler_params=pltpu.CompilerParams(collective_id=0, has_side_effects=True),
    )(
        key_lists.reshape(local, slots),
        list_len.reshape(local),
        tokens.reshape(rows, width),
        w_qkv,
    )
    mixed = jnp.dot(attn, w_out, preferred_element_type=jnp.float32).astype(jnp.bfloat16)
    return mixed.reshape(1, rows, width)


def solution(mesh):
    sizes = (mesh.shape["view"], mesh.shape["half"])
    placed = (
        P(("scene", "view"), "half", None),
        P(),
        P(),
        P(("scene", "view"), "half", None),
        P(("scene", "view"), "half"),
    )
    return jax.shard_map(
        functools.partial(per_device, sizes),
        mesh=mesh,
        in_specs=placed,
        out_specs=P(("scene", "view"), "half", None),
        check_vma=False,
    )
```

```python
import functools

import jax
import jax.numpy as jnp
from jax import lax
from jax.experimental import pallas as pl
from jax.experimental.pallas import tpu as pltpu
from jax.sharding import PartitionSpec as P

HEADS = 4
NEG = -1e30
MESH = pl.DeviceIdType.MESH


def body(
    sizes,
    lists_ref,
    lens_ref,
    tokens_ref,
    w_ref,
    out_ref,
    x,
    w,
    kbuf,
    vbuf,
    weight_buf,
    total_buf,
    load_sem,
    send_sem,
    recv_sem,
):
    views, halves = sizes
    view, half = lax.axis_index("view"), lax.axis_index("half")
    count, block, inner = kbuf.shape
    local = count // (views * halves)
    rows = local * block
    head_size = inner // HEADS
    slots = lists_ref.shape[1]
    bufs = (kbuf, vbuf)

    loads = [pltpu.make_async_copy(tokens_ref, x, load_sem.at[0])]
    for n, group in enumerate((1, 2, 0)):
        cols = pl.ds(group * inner, inner)
        loads.append(
            pltpu.make_async_copy(w_ref.at[:, cols], w.at[group], load_sem.at[1 + n])
        )
    for load in loads:
        load.start()

    toward = (
        (view + 1 < views, {"view": view + 1}, views),
        (view >= 1, {"view": view - 1}, views),
        (half + 1 < halves, {"half": half + 1}, halves),
        (half >= 1, {"half": half - 1}, halves),
    )

    barrier = pltpu.get_barrier_semaphore()
    for there, device, size in toward:
        if size > 1:

            @pl.when(there)
            def _():
                pl.semaphore_signal(barrier, inc=1, device_id=device, device_id_type=MESH)

    def piece(c, slot, way):
        rows_of = bufs[c].at[slot]
        return pltpu.make_async_remote_copy(
            src_ref=rows_of,
            dst_ref=rows_of,
            send_sem=send_sem.at[way, c, slot],
            recv_sem=recv_sem.at[c, slot],
            device_id=toward[way][1],
            device_id_type=MESH,
        )

    sends = []

    def send(c, slot, way, here):
        there, _, size = toward[way]
        if size == 1:
            return
        cond = there if here is None else jnp.logical_and(here, there)
        sends.append((cond, c, slot, way))

        @pl.when(cond)
        def _():
            piece(c, slot, way).start()

    def arrive(c, slot, here):
        @pl.when(here)
        def _():
            piece(c, slot, 0).wait_recv()

    def project(group):
        return jnp.dot(x[...], w[group], preferred_element_type=jnp.float32).astype(
            jnp.bfloat16
        )

    own = view * halves + half
    loads[0].wait()
    for c in range(2):
        loads[1 + c].wait()
        bufs[c][pl.ds(own * local, local)] = project(1 + c).reshape(local, block, inner)
        if c == 0:
            expected = sum(there.astype(jnp.int32) for there, _, size in toward if size > 1)
            pl.semaphore_wait(barrier, expected)
        for b in range(local):
            for way in (2, 3, 0, 1):
                send(c, own * local + b, way, None)

    loads[3].wait()
    queries = project(0)
    head_of = lax.broadcasted_iota(jnp.int32, (block, inner), 1) // head_size
    mine = [head_of == h for h in range(HEADS)]

    balanced = halves == 2 and views > 2
    last = views - 1

    def along_view(c, dist):
        for b in range(local):
            for sign, way in ((-1, 0), (1, 1)):
                shard = view + sign * dist
                here = shard >= 0 if sign < 0 else shard < views
                slot = (shard * halves + half) * local + b
                arrive(c, slot, here)
                across = here
                if balanced and c == 1:
                    across = shard >= 1 if sign < 0 else shard < last
                for out in (2, 3):
                    send(c, slot, out, across)
                if dist + 1 < views:
                    send(c, slot, way, here)

    def relay(dist):
        for b in range(local):
            for shard, here, way in ((0, view == dist, 0), (last, view == last - dist, 1)):
                slot = (shard * halves + (halves - 1) - half) * local + b
                arrive(1, slot, here)
                if dist < last:
                    send(1, slot, way, here)

    def along_half(c):
        for far in range(1, halves):
            for dist in range(views):
                for b in range(local):
                    for sign in (-1, 1) if dist else (1,):
                        shard = view + sign * dist
                        seen = shard >= 0 if sign < 0 else shard < views
                        if balanced and c == 1:
                            seen = jnp.logical_and(shard >= 1, shard < last)
                        for side, way in ((-1, 2), (1, 3)):
                            other = half + side * far
                            here = jnp.logical_and(
                                seen, other >= 0 if side < 0 else other < halves
                            )
                            slot = (shard * halves + other) * local + b
                            arrive(c, slot, here)
                            if far + 1 < halves:
                                send(c, slot, way, here)

    for dist in range(1, views):
        along_view(0, dist)
        if balanced and dist > 1:
            relay(dist - 1)
        along_view(1, dist)
        if balanced and dist == 1:
            relay(0)

    along_half(0)
    for i in range(local):
        q = queries[i * block : (i + 1) * block]
        stacked = jnp.concatenate([jnp.where(m, q, jnp.zeros_like(q)) for m in mine], axis=0)
        keys = jnp.concatenate([kbuf[lists_ref[i, s]] for s in range(slots)], axis=0)
        scores = lax.dot_general(
            stacked, keys, (((1,), (1,)), ((), ())), preferred_element_type=jnp.float32
        ) * head_size ** (-0.5)
        live = lax.broadcasted_iota(jnp.int32, scores.shape, 1) // block < lens_ref[i]
        top = jnp.max(jnp.where(live, scores, NEG), axis=1, keepdims=True)
        weights = jnp.where(live, jnp.exp(scores - top), 0.0)
        total_buf[i] = jnp.sum(weights, axis=1, keepdims=True)
        weight_buf[i] = weights.astype(jnp.bfloat16)

    along_half(1)
    if balanced:
        relay(last)
    for i in range(local):
        values = jnp.concatenate([vbuf[lists_ref[i, s]] for s in range(slots)], axis=0)
        summed = jnp.dot(weight_buf[i], values, preferred_element_type=jnp.float32)
        scaled = summed / total_buf[i]
        attn = jnp.zeros((block, inner), jnp.float32)
        for h, m in enumerate(mine):
            attn = jnp.where(m, scaled[h * block : (h + 1) * block], attn)
        out_ref[i * block : (i + 1) * block] = attn.astype(out_ref.dtype)

    for cond, c, slot, way in sends:

        @pl.when(cond)
        def _():
            piece(c, slot, way).wait_send()


def per_device(sizes, tokens, w_qkv, w_out, key_lists, list_len):
    views, halves = sizes
    rows, width = tokens.shape[1:]
    inner = w_out.shape[0]
    local = key_lists.shape[1]
    slots = key_lists.shape[2]
    block = rows // local
    shards = views * halves
    anywhere = pl.BlockSpec(memory_space=pl.ANY)
    attn = pl.pallas_call(
        functools.partial(body, sizes),
        out_shape=jax.ShapeDtypeStruct((rows, inner), jnp.bfloat16),
        in_specs=[
            pl.BlockSpec(memory_space=pltpu.SMEM),
            pl.BlockSpec(memory_space=pltpu.SMEM),
            anywhere,
            anywhere,
        ],
        out_specs=pl.BlockSpec(memory_space=pltpu.VMEM),
        scratch_shapes=[
            pltpu.VMEM((rows, width), jnp.bfloat16),
            pltpu.VMEM((3, width, inner), jnp.bfloat16),
            pltpu.VMEM((shards * local, block, inner), jnp.bfloat16),
            pltpu.VMEM((shards * local, block, inner), jnp.bfloat16),
            pltpu.VMEM((local, HEADS * block, slots * block), jnp.bfloat16),
            pltpu.VMEM((local, HEADS * block, 1), jnp.float32),
            pltpu.SemaphoreType.DMA((4,)),
            pltpu.SemaphoreType.DMA((4, 2, shards * local)),
            pltpu.SemaphoreType.DMA((2, shards * local)),
        ],
        compiler_params=pltpu.CompilerParams(collective_id=0, has_side_effects=True),
    )(
        key_lists.reshape(local, slots),
        list_len.reshape(local),
        tokens.reshape(rows, width),
        w_qkv,
    )
    mixed = jnp.dot(attn, w_out, preferred_element_type=jnp.float32).astype(jnp.bfloat16)
    return mixed.reshape(1, rows, width)


def solution(mesh):
    sizes = (mesh.shape["view"], mesh.shape["half"])
    placed = (
        P(("scene", "view"), "half", None),
        P(),
        P(),
        P(("scene", "view"), "half", None),
        P(("scene", "view"), "half"),
    )
    return jax.shard_map(
        functools.partial(per_device, sizes),
        mesh=mesh,
        in_specs=placed,
        out_specs=P(("scene", "view"), "half", None),
        check_vma=False,
    )
```

```python
import functools

import jax
import jax.numpy as jnp
from jax import lax
from jax.experimental import pallas as pl
from jax.experimental.pallas import tpu as pltpu
from jax.sharding import PartitionSpec as P

HEADS = 4
NEG = -1e30
MESH = pl.DeviceIdType.MESH


def body(
    sizes,
    lists_ref,
    lens_ref,
    tokens_ref,
    w_ref,
    out_ref,
    x,
    w,
    kbuf,
    vbuf,
    weight_buf,
    total_buf,
    load_sem,
    send_sem,
    recv_sem,
):
    views, halves = sizes
    view, half = lax.axis_index("view"), lax.axis_index("half")
    count, block, inner = kbuf.shape
    local = count // (views * halves)
    rows = local * block
    head_size = inner // HEADS
    slots = lists_ref.shape[1]
    bufs = (kbuf, vbuf)

    loads = [pltpu.make_async_copy(tokens_ref, x, load_sem.at[0])]
    for n, group in enumerate((1, 2, 0)):
        cols = pl.ds(group * inner, inner)
        loads.append(
            pltpu.make_async_copy(w_ref.at[:, cols], w.at[group], load_sem.at[1 + n])
        )
    for load in loads[:2]:
        load.start()

    toward = (
        (view + 1 < views, {"view": view + 1}, views),
        (view >= 1, {"view": view - 1}, views),
        (half + 1 < halves, {"half": half + 1}, halves),
        (half >= 1, {"half": half - 1}, halves),
    )

    barrier = pltpu.get_barrier_semaphore()
    for there, device, size in toward:
        if size > 1:

            @pl.when(there)
            def _():
                pl.semaphore_signal(barrier, inc=1, device_id=device, device_id_type=MESH)

    def piece(c, slot, way):
        rows_of = bufs[c].at[slot]
        return pltpu.make_async_remote_copy(
            src_ref=rows_of,
            dst_ref=rows_of,
            send_sem=send_sem.at[way, c, slot],
            recv_sem=recv_sem.at[c, slot],
            device_id=toward[way][1],
            device_id_type=MESH,
        )

    sends = []

    def send(c, slot, way, here):
        there, _, size = toward[way]
        if size == 1:
            return
        cond = there if here is None else jnp.logical_and(here, there)
        sends.append((cond, c, slot, way))

        @pl.when(cond)
        def _():
            piece(c, slot, way).start()

    def arrive(c, slot, here):
        @pl.when(here)
        def _():
            piece(c, slot, 0).wait_recv()

    def project(group):
        return jnp.dot(x[...], w[group], preferred_element_type=jnp.float32).astype(
            jnp.bfloat16
        )

    own = view * halves + half
    loads[0].wait()
    for c in range(2):
        loads[1 + c].wait()
        loads[2 + c].start()
        for b in range(local):
            bufs[c][own * local + b] = jnp.dot(
                x[b * block : (b + 1) * block], w[1 + c], preferred_element_type=jnp.float32
            ).astype(jnp.bfloat16)
            if c == 0 and b == 0:
                expected = sum(there.astype(jnp.int32) for there, _, size in toward if size > 1)
                pl.semaphore_wait(barrier, expected)
            for way in (2, 3, 0, 1):
                send(c, own * local + b, way, None)

    loads[3].wait()
    queries = project(0)
    head_of = lax.broadcasted_iota(jnp.int32, (block, inner), 1) // head_size
    mine = [head_of == h for h in range(HEADS)]

    balanced = halves == 2 and views > 2
    last = views - 1

    def along_view(c, dist):
        for b in range(local):
            for sign, way in ((-1, 0), (1, 1)):
                shard = view + sign * dist
                here = shard >= 0 if sign < 0 else shard < views
                slot = (shard * halves + half) * local + b
                arrive(c, slot, here)
                across = here
                if balanced and c == 1:
                    across = shard >= 1 if sign < 0 else shard < last
                for out in (2, 3):
                    send(c, slot, out, across)
                if dist + 1 < views:
                    send(c, slot, way, here)

    def relay(dist):
        for b in range(local):
            for shard, here, way in ((0, view == dist, 0), (last, view == last - dist, 1)):
                slot = (shard * halves + (halves - 1) - half) * local + b
                arrive(1, slot, here)
                if dist < last:
                    send(1, slot, way, here)

    def along_half(c):
        for far in range(1, halves):
            for dist in range(views):
                for b in range(local):
                    for sign in (-1, 1) if dist else (1,):
                        shard = view + sign * dist
                        seen = shard >= 0 if sign < 0 else shard < views
                        if balanced and c == 1:
                            seen = jnp.logical_and(shard >= 1, shard < last)
                        for side, way in ((-1, 2), (1, 3)):
                            other = half + side * far
                            here = jnp.logical_and(
                                seen, other >= 0 if side < 0 else other < halves
                            )
                            slot = (shard * halves + other) * local + b
                            arrive(c, slot, here)
                            if far + 1 < halves:
                                send(c, slot, way, here)

    for dist in range(1, views):
        along_view(0, dist)
        if balanced and dist > 1:
            relay(dist - 1)
        along_view(1, dist)
        if balanced and dist == 1:
            relay(0)

    along_half(0)
    for i in range(local):
        q = queries[i * block : (i + 1) * block]
        stacked = jnp.concatenate([jnp.where(m, q, jnp.zeros_like(q)) for m in mine], axis=0)
        keys = jnp.concatenate([kbuf[lists_ref[i, s]] for s in range(slots)], axis=0)
        scores = lax.dot_general(
            stacked, keys, (((1,), (1,)), ((), ())), preferred_element_type=jnp.float32
        ) * head_size ** (-0.5)
        live = lax.broadcasted_iota(jnp.int32, scores.shape, 1) // block < lens_ref[i]
        top = jnp.max(jnp.where(live, scores, NEG), axis=1, keepdims=True)
        weights = jnp.where(live, jnp.exp(scores - top), 0.0)
        total_buf[i] = jnp.sum(weights, axis=1, keepdims=True)
        weight_buf[i] = weights.astype(jnp.bfloat16)

    along_half(1)
    if balanced:
        relay(last)
    for i in range(local):
        values = jnp.concatenate([vbuf[lists_ref[i, s]] for s in range(slots)], axis=0)
        summed = jnp.dot(weight_buf[i], values, preferred_element_type=jnp.float32)
        scaled = summed / total_buf[i]
        attn = jnp.zeros((block, inner), jnp.float32)
        for h, m in enumerate(mine):
            attn = jnp.where(m, scaled[h * block : (h + 1) * block], attn)
        out_ref[i * block : (i + 1) * block] = attn.astype(out_ref.dtype)

    for cond, c, slot, way in sends:

        @pl.when(cond)
        def _():
            piece(c, slot, way).wait_send()


def per_device(sizes, tokens, w_qkv, w_out, key_lists, list_len):
    views, halves = sizes
    rows, width = tokens.shape[1:]
    inner = w_out.shape[0]
    local = key_lists.shape[1]
    slots = key_lists.shape[2]
    block = rows // local
    shards = views * halves
    anywhere = pl.BlockSpec(memory_space=pl.ANY)
    attn = pl.pallas_call(
        functools.partial(body, sizes),
        out_shape=jax.ShapeDtypeStruct((rows, inner), jnp.bfloat16),
        in_specs=[
            pl.BlockSpec(memory_space=pltpu.SMEM),
            pl.BlockSpec(memory_space=pltpu.SMEM),
            anywhere,
            anywhere,
        ],
        out_specs=pl.BlockSpec(memory_space=pltpu.VMEM),
        scratch_shapes=[
            pltpu.VMEM((rows, width), jnp.bfloat16),
            pltpu.VMEM((3, width, inner), jnp.bfloat16),
            pltpu.VMEM((shards * local, block, inner), jnp.bfloat16),
            pltpu.VMEM((shards * local, block, inner), jnp.bfloat16),
            pltpu.VMEM((local, HEADS * block, slots * block), jnp.bfloat16),
            pltpu.VMEM((local, HEADS * block, 1), jnp.float32),
            pltpu.SemaphoreType.DMA((4,)),
            pltpu.SemaphoreType.DMA((4, 2, shards * local)),
            pltpu.SemaphoreType.DMA((2, shards * local)),
        ],
        compiler_params=pltpu.CompilerParams(collective_id=0, has_side_effects=True),
    )(
        key_lists.reshape(local, slots),
        list_len.reshape(local),
        tokens.reshape(rows, width),
        w_qkv,
    )
    mixed = jnp.dot(attn, w_out, preferred_element_type=jnp.float32).astype(jnp.bfloat16)
    return mixed.reshape(1, rows, width)


def solution(mesh):
    sizes = (mesh.shape["view"], mesh.shape["half"])
    placed = (
        P(("scene", "view"), "half", None),
        P(),
        P(),
        P(("scene", "view"), "half", None),
        P(("scene", "view"), "half"),
    )
    return jax.shard_map(
        functools.partial(per_device, sizes),
        mesh=mesh,
        in_specs=placed,
        out_specs=P(("scene", "view"), "half", None),
        check_vma=False,
    )
```
